32 devices in a mesh: dom: 16 (over z, y, x), orb: 2 (over core).
Axes of the slice: x: 2, y: 2, z: 4, core: 2. Of those that a mesh axis runs over, the one named last changes fastest.
Arguments:
- orbitals: bfloat16 [768, 64, 512], P('dom', 'orb'), may hold values from -6 to 6
- adjoint_source: bfloat16 [768, 64, 512], P('dom', 'orb'), may hold values from -6 to 6
- eigenvalues: float32 [64], P('orb'), may hold values from -1 to -0.25
- cell_scale: float32 [768], P('dom'), may hold values from 0.4 to 1.6
- base_potential: float32 [768, 512], P('dom'), may hold values from 0.5 to 1.5
- stiffness: bfloat16 [512, 512], replicated, may hold values from -1.5 to 1.5, as said below
- face_perm: int32 [768, 64], P('dom'), may hold values from 0 to 63, each once within a row
- restrict: bfloat16 [512, 64], replicated, may hold values from -0.25 to 0.25
- prolong: bfloat16 [64, 512], replicated, may hold values from -0.75 to 0.75
- owner: int32 [768, 1], P('dom'), may hold values from 0 to 15; in each aligned block of 48 rows (0 to 47, 48 to 95, ...) at most 6 rows name the same one
- pot_slot: int32 [768], P('dom'), may hold values from 0 to 63
- potential: float32 [1024, 64], P('dom'), may hold values from -6 to 6
Outputs:
- adjoint: bfloat16 [768, 64, 512], P('dom', 'orb')
- updated: float32 [1024, 64], P('dom')
- applied: bfloat16 [768, 64, 512], P('dom', 'orb')
The draws below stay inside these ranges and needn't reach their ends.
Inputs may be any that keep to these rules, and one draw needn't show every extreme that they name: In the rows of one device no owner is named by more than 6 cells. `face_perm`: each row is a permutation. `stiffness`: symmetric.
All inputs are finite; a program needn't handle non-finite values.
Results may differ from the reference program's by a relative error of at most 0.0027.
Values sent between devices are 32-bit elements; how exact they have to be, the bound alone decides.
A program may use at most 64 MiB of HBM per device.

```python
import math
import jax
import jax.numpy as jnp
import numpy as np
from jax import lax

P_SIZE = 512
FACE = 64
PN = 64
ORB = 64
CELL_DEV = 48
CELLS = 768
POT_DEV = 64
POT_CELLS = 1024
CAP = 6
ITERS = 4
N_DOM = 16


def draw_stiffness(key, part):
    key_diag, key_noise = jax.random.split(jax.random.fold_in(key, 11))
    diagonal = jax.random.uniform(key_diag, (P_SIZE,), jnp.float32, 0.8, 1.2)
    noise = jax.random.normal(key_noise, (P_SIZE, P_SIZE), jnp.float32) * (0.25 / P_SIZE ** 0.5)
    symmetric = (noise + noise.T) * 0.5 ** 0.5
    return (symmetric + jnp.diag(diagonal)).astype(jnp.bfloat16)


def plant(values, own_key, least, top_value):
    dims = values.shape
    spot = [jax.random.randint(jax.random.fold_in(own_key, axis), (), 0, dims[axis]) for axis in range(len(dims))]
    values = values.at[tuple(spot)].set(least)
    longest = dims.index(max(dims))
    spot[longest] = (spot[longest] + 1) % dims[longest]
    return values.at[tuple(spot)].set(top_value)


def block_levels(own_key, shape, cuts, smallest, top_value):
    def one(axis_at, blocks):
        heights = jax.random.uniform(jax.random.fold_in(jax.random.fold_in(own_key, 6), axis_at), (blocks,), jnp.float32, smallest / len(cuts), top_value / len(cuts))
        return jnp.repeat(jnp.exp(heights), shape[axis_at] // blocks).reshape((-1,) + (1,) * (len(shape) - axis_at - 1))

    factor_of = one(*cuts[0])
    for cut in cuts[1:]:
        factor_of = factor_of * one(*cut)
    return factor_of


def assign_block(own_key, own, number, rows, number_of, top, bound, skew):
    ranking = jax.random.permutation(own_key, number_of)
    packed, common = load_shares(number_of, rows * top, bound, skew, True), load_shares(number_of, rows * top, bound, skew, False)
    places = jnp.arange(number_of)

    def named(tallies, offset_by):
        used = int((tallies > 0).sum())
        fixed = max(1, used // 4)
        passed = fixed + (places - fixed + offset_by * (used - fixed)) % max(1, number_of - fixed)
        return jnp.zeros((number_of,), jnp.int32).at[ranking[jnp.where(places < fixed, places, passed)]].set(jnp.asarray(tallies, jnp.int32))

    tallies = jnp.where(number % 4 == 0, named(packed, number // 4), named(common, number - number // 4 - 1))
    mixed = jax.random.permutation(jax.random.fold_in(own, 3), number_of)
    source_of, receiver = mixed[0:number_of // 2 * 2:2], mixed[1:number_of // 2 * 2:2]
    room = jnp.minimum(tallies[source_of] - 1, bound - tallies[receiver]) // 2
    room = jnp.where((source_of == ranking[0]) | (receiver == ranking[0]) | (tallies[receiver] == 0), 0, jnp.maximum(room, 0))
    passed = jax.random.randint(jax.random.fold_in(own, 4), (number_of // 2,), 0, 1 << 20) % (room + 1)
    tallies = tallies.at[source_of].add(-passed).at[receiver].add(passed)
    members = jnp.searchsorted(jnp.cumsum(tallies), jnp.arange(rows * top), side="right").astype(jnp.int32)
    table = members.reshape(top, rows).T
    table = table[jax.random.permutation(jax.random.fold_in(own, 1), rows)]
    offset_by = jax.random.randint(jax.random.fold_in(own, 2), (rows, 1), 0, top)
    return jnp.take_along_axis(table, (jnp.arange(top)[None, :] + offset_by) % top, axis=1)


def load_shares(number_of, total, bound, slope, full):
    loads = [(1 << 20) // math.isqrt(rank ** slope) + 1 for rank in range(1, number_of + 1)]
    largest = bound if full else min(bound, max(-(-total // number_of), total * loads[0] // sum(loads)))
    least = 1 if total - largest >= number_of - 1 else 0
    holding, spare = [largest] + [least] * (number_of - 1), total - largest - least * (number_of - 1)
    while spare > 0:
        free = [i for i in range(1, number_of) if holding[i] < largest] or [i for i in range(1, number_of) if holding[i] < bound]
        pool, budget = sum([loads[i] for i in free]), spare
        for i in free:
            addition = min(bound - holding[i], max(1, budget * loads[i] // pool), spare)
            holding[i] = holding[i] + addition
            spare = spare - addition
    return np.array(holding)


def normal_values(key, extent, spread, reach, shards=(), kind=jnp.bfloat16):
    loudness = block_levels(key, extent, shards, -0.22, 0.18) if shards else 1.0
    values = jax.random.normal(key, extent, jnp.float32) * spread * loudness
    return jnp.minimum(jnp.maximum(values, -reach), reach).astype(kind)


def setup_inputs(seed: int = 0) -> dict:
    keys = jax.random.split(jax.random.key(seed), 13)
    orbitals = normal_values(keys[0], (CELLS, ORB, P_SIZE), 1.0, 6.0, ((0, 16), (1, 2)))
    adjoint_source = normal_values(keys[1], (CELLS, ORB, P_SIZE), 1.0, 6.0, ((0, 16), (1, 2)))
    eigenvalues = jnp.clip(-1.0 + 0.75 * jax.random.uniform(keys[2], (ORB,), jnp.float32) ** block_levels(keys[2], (ORB,), ((0, 2),), -0.2, 0.2), -1.0, -0.25)
    cell_scale = jnp.clip(jnp.exp(math.log(1.6) - 1.3862944 * jax.random.uniform(keys[3], (CELLS,), jnp.float32) ** block_levels(keys[3], (CELLS,), ((0, 16),), -0.2, 0.2)), 0.4, 1.6)
    base_potential = jnp.clip(0.5 + 1.0 * jax.random.uniform(keys[4], (CELLS, P_SIZE), jnp.float32) ** block_levels(keys[4], (CELLS, P_SIZE), ((0, 16),), -0.2, 0.2), 0.5, 1.5)
    stiffness = draw_stiffness(jax.random.fold_in(keys[12], 71), 0)
    face_perm = jax.vmap(lambda own: jax.random.permutation(own, FACE))(jax.random.split(keys[6], CELLS)).reshape((CELLS, FACE)).astype(jnp.int32)
    restrict = normal_values(keys[7], (P_SIZE, PN), P_SIZE ** -0.5, 0.25)
    prolong = normal_values(keys[8], (PN, P_SIZE), PN ** -0.5, 0.75)
    owner_keys = jax.random.split(jax.random.fold_in(keys[9], 1), CELLS // CELL_DEV)
    owner_turns = jax.random.permutation(jax.random.fold_in(keys[9], 3), CELLS // CELL_DEV)
    owner = jax.vmap(lambda own, number: assign_block(jax.random.fold_in(keys[9], 2), own, number, CELL_DEV, N_DOM, 1, CAP, 2))(owner_keys, owner_turns).reshape((CELLS, 1))
    pot_slot = plant(jax.random.randint(keys[10], (CELLS,), 0, POT_DEV), jax.random.fold_in(keys[10], 1), 0, POT_DEV - 1).astype(jnp.int32)
    potential = normal_values(keys[11], (POT_CELLS, PN), 1.0, 6.0, ((0, 16),), jnp.float32)
    return dict(orbitals=orbitals, adjoint_source=adjoint_source, eigenvalues=eigenvalues, cell_scale=cell_scale, base_potential=base_potential, stiffness=stiffness, face_perm=face_perm, restrict=restrict, prolong=prolong, owner=owner, pot_slot=pot_slot, potential=potential)


relax = 0.25
step_rate = 0.1


def face_onehot(face_perm):
    faces = face_perm.shape[1]
    return (face_perm[:, :, None] == jnp.arange(faces, dtype=jnp.int32)[None, None, :]).astype(jnp.float32)


def assemble(partial_sum, onehot):
    faces = onehot.shape[1]
    nodes = partial_sum.shape[2]
    left_face = partial_sum[:, :, :faces]
    right_face = partial_sum[:, :, nodes - faces:]
    sent_right = jnp.einsum('ckj,cok->coj', onehot, right_face, precision=lax.Precision.HIGHEST)
    zero_face = jnp.zeros_like(left_face[:1])
    left_next = jnp.concatenate([left_face[1:], zero_face], 0)
    add_right = jnp.einsum('ckj,coj->cok', onehot, left_next, precision=lax.Precision.HIGHEST)
    add_left = jnp.concatenate([zero_face, sent_right[:-1]], 0)
    return jnp.concatenate([left_face + add_left, partial_sum[:, :, faces:nodes - faces], right_face + add_right], 2)


def cell_operator(values_bf, values_full, shift, cell_scale, stiffness, onehot):
    nodes = stiffness.shape[0]
    kinetic = jnp.dot(values_bf.reshape(-1, nodes), stiffness, preferred_element_type=jnp.float32).reshape(values_full.shape)
    partial_sum = cell_scale[:, None, None] * kinetic + shift * values_full
    return assemble(partial_sum, onehot)


def reference(orbitals, adjoint_source, eigenvalues, cell_scale, base_potential, stiffness, face_perm, restrict, prolong, owner, pot_slot, potential):
    onehot = face_onehot(face_perm)
    width = min(8, ORB)
    blocks = ORB // width

    def solve_block(index):
        start = (index * width).astype(jnp.int32)
        psi_block = lax.dynamic_slice_in_dim(orbitals, start, width, 1)
        source_block = lax.dynamic_slice_in_dim(adjoint_source, start, width, 1).astype(jnp.float32)
        eig_block = lax.dynamic_slice_in_dim(eigenvalues, start, width, 0)
        shift = base_potential[:, None, :] - eig_block[None, :, None]
        iterate = relax * source_block
        for step_index in range(ITERS):
            image = cell_operator(iterate.astype(jnp.bfloat16), iterate, shift, cell_scale, stiffness, onehot)
            iterate = iterate + relax * (source_block - image)
        product = jnp.sum(psi_block.astype(jnp.float32) * iterate, axis=1)
        return iterate.astype(jnp.bfloat16), product

    adjoint_blocks, products = lax.map(solve_block, jnp.arange(blocks, dtype=jnp.int32))
    adjoint = jnp.transpose(adjoint_blocks, (1, 0, 2, 3)).reshape(CELLS, ORB, P_SIZE)
    density_term = jnp.sum(products, 0)
    projected = jnp.dot(density_term, restrict.astype(jnp.float32), precision=lax.Precision.HIGHEST)
    target = (owner[:, 0] * POT_DEV + pot_slot).astype(jnp.int32)
    summed = jax.ops.segment_sum(projected, target, num_segments=POT_DEV * N_DOM)
    updated = potential - step_rate * summed
    cell_pot = updated[target]
    node_potential = jnp.dot(cell_pot, prolong.astype(jnp.float32), precision=lax.Precision.HIGHEST)
    shift_new = (base_potential + node_potential)[:, None, :]

    def apply_block(index):
        start = (index * width).astype(jnp.int32)
        psi_block = lax.dynamic_slice_in_dim(orbitals, start, width, 1)
        result = cell_operator(psi_block, psi_block.astype(jnp.float32), shift_new, cell_scale, stiffness, onehot)
        return result.astype(jnp.bfloat16)

    applied_blocks = lax.map(apply_block, jnp.arange(blocks, dtype=jnp.int32))
    applied = jnp.transpose(applied_blocks, (1, 0, 2, 3)).reshape(CELLS, ORB, P_SIZE)
    return adjoint, updated, applied
```

```python
import functools

import jax
import jax.numpy as jnp
from jax import lax
from jax.experimental import pallas as pl
from jax.experimental.pallas import tpu as pltpu
from jax.sharding import PartitionSpec as P

ITERS = 4


relax = 0.25
step_rate = 0.1

LANES = 128
F32 = jnp.float32
BF16 = jnp.bfloat16


def split(x):
    hi = x.astype(BF16)
    return hi, (x - hi.astype(F32)).astype(BF16)


def dot(a, b):
    return jnp.dot(a, b, preferred_element_type=F32)


def dot_first(a, b):
    return lax.dot_general(a, b, (((0,), (0,)), ((), ())), preferred_element_type=F32)


def kernel(
    n,
    ranks,
    psi,
    src,
    eig,
    scale,
    base,
    stiff,
    idx,
    early,
    restrict,
    prolong,
    pot,
    adj,
    upd,
    app,
    it,
    kin,
    face0,
    face3,
    dens,
    tx_l,
    tx_r,
    rx_l,
    rx_r,
    ex_tl,
    ex_tr,
    ex_l,
    ex_r,
    early_all,
    rows_all,
    own,
    mt_lo,
    mt_hi,
    tcols,
    tturn,
    packed,
    packed_in,
    node,
    hs_l,
    hs_r,
    hr_l,
    hr_r,
    xs,
    xr,
    es,
    er,
    ps,
    pr,
    ws,
    wr,
):
    cells, orbs, nodes = psi.shape
    half = cells // 2
    prow = pot.shape[0]
    phalf = prow // 2
    coarse = pot.shape[1]
    last = nodes - LANES
    d = lax.axis_index("dom")
    r = lax.axis_index("orb")
    barrier = pltpu.get_barrier_semaphore()

    def greet_dom(k, carry):
        pl.semaphore_signal(barrier, inc=1, device_id={"dom": lax.rem(d + k, n)}, device_id_type=pl.DeviceIdType.MESH)
        return carry

    def greet_orb(k, carry):
        pl.semaphore_signal(barrier, inc=1, device_id={"orb": lax.rem(r + k, ranks)}, device_id_type=pl.DeviceIdType.MESH)
        return carry

    lax.fori_loop(1, n, greet_dom, 0)
    lax.fori_loop(1, ranks, greet_orb, 0)

    def send(source, target, s, t, where):
        return pltpu.make_async_remote_copy(
            src_ref=source,
            dst_ref=target,
            send_sem=s,
            recv_sem=t,
            device_id=where,
            device_id_type=pl.DeviceIdType.MESH,
        )

    right = {"dom": jnp.minimum(d + 1, n - 1)}
    left = {"dom": jnp.maximum(d - 1, 0)}
    has_right = d < n - 1
    has_left = d > 0

    def to_left(t):
        return send(tx_l.at[t], rx_r.at[t], hs_l.at[t], hr_r.at[t], left)

    def to_right(t):
        return send(tx_r.at[t], rx_l.at[t], hs_r.at[t], hr_l.at[t], right)

    x_left = send(ex_tl, ex_r, xs.at[0], xr.at[0], left)
    x_right = send(ex_tr, ex_l, xs.at[1], xr.at[1], right)

    def early_copy(k):
        return send(early, early_all.at[d], es.at[k], er.at[k], {"dom": lax.rem(d + k, n)})

    def rows_copy(k):
        return send(own, rows_all.at[d], ps.at[k], pr.at[k], {"dom": lax.rem(d + k, n)})

    def rank_copy(k):
        return send(packed, packed_in.at[k], ws.at[k], wr.at[k], {"orb": lax.rem(r + k, ranks)})

    lane = lax.broadcasted_iota(jnp.int32, (orbs, LANES), 1)
    low = lane < LANES // 2

    def turned(x, row):
        return jnp.take_along_axis(x, jnp.broadcast_to(row, (orbs, LANES)), axis=1)

    group = 8 if cells % 8 == 0 else 1

    def init(c, carry):
        it[c] = relax * src[c].astype(F32)
        return carry

    lax.fori_loop(0, cells, init, 0, unroll=4)

    def apply_group(g, carry):
        block = psi[pl.ds(g * group, group)].astype(F32).reshape(group * orbs, nodes).astype(BF16)
        product = dot(block, stiff[...])
        for k in range(group):
            c = g * group + k
            part = product[k * orbs : (k + 1) * orbs]
            kin[c] = scale[c] * part + base[pl.ds(c, 1), :] * psi[c].astype(F32)
        return carry

    def step_group(g, carry):
        block = it[pl.ds(g * group, group)].reshape(group * orbs, nodes).astype(BF16)
        product = dot(block, stiff[...])
        for k in range(group):
            c = g * group + k
            value = it[c]
            part = scale[c] * product[k * orbs : (k + 1) * orbs] + (base[pl.ds(c, 1), :] - eig[...]) * value
            it[c] = value + relax * (src[c].astype(F32) - part)
            face0[c] = part[:, :LANES]
            face3[c] = part[:, last:]
        return carry

    def inner_face(c, carry):
        y = turned(jnp.where(low, face0[c + 1], face3[c]), idx[pl.ds(c, 1), :])
        it[c + 1, :, :LANES] = it[c + 1, :, :LANES] - relax * jnp.where(low, y, 0.0)
        it[c, :, last:] = it[c, :, last:] - relax * jnp.where(low, 0.0, y)
        return carry

    end = cells - 1
    shares = -(-(n - 1) // max(1, ITERS - 1))
    for t in range(ITERS):
        edge = it[0]
        tx_l[t] = scale[0] * dot(edge.astype(BF16), stiff[:, :LANES]) + (base[0:1, :LANES] - eig[...]) * edge[:, :LANES]
        edge = it[end]
        part = scale[end] * dot(edge.astype(BF16), stiff[:, last:]) + (base[end : end + 1, last:] - eig[...]) * edge[:, last:]
        tx_r[t] = turned(part, idx[end : end + 1, :])
        if t == 0:
            pl.semaphore_wait(barrier, n - 1 + ranks - 1)

        @pl.when(has_left)
        def _():
            to_left(t).start()

        @pl.when(has_right)
        def _():
            to_right(t).start()

        def send_early(k, carry):
            early_copy(k).start()
            return carry

        lax.fori_loop(min(n, 1 + t * shares), min(n, 1 + (t + 1) * shares), send_early, 0)
        lax.fori_loop(0, cells // group, step_group, 0)
        lax.fori_loop(0, end, inner_face, 0, unroll=2)
        if t == 0:
            lax.fori_loop(0, cells // group, apply_group, 0)
            ex_tl[:orbs] = kin[0, :, :LANES]
            ex_tl[orbs:] = psi[0].astype(F32)[:, :LANES]
            ex_tr[:orbs] = kin[end, :, last:]
            ex_tr[orbs : 2 * orbs] = psi[end].astype(F32)[:, last:]
            ex_tr[2 * orbs :] = jnp.broadcast_to(idx[end : end + 1, :], (8, LANES)).astype(F32)

            @pl.when(has_left)
            def _():
                x_left.start()

            @pl.when(has_right)
            def _():
                x_right.start()

        @pl.when(has_left)
        def _():
            to_right(t).wait_recv()
            it[0, :, :LANES] = it[0, :, :LANES] - relax * jnp.where(low, rx_l[t], 0.0)

        @pl.when(has_right)
        def _():
            to_left(t).wait_recv()
            y = turned(rx_r[t], idx[end : end + 1, :])
            it[end, :, last:] = it[end, :, last:] - relax * jnp.where(low, 0.0, y)

    def finish(c, carry):
        dens[pl.ds(c, 1), :] = jnp.sum(psi[c].astype(F32) * it[c], axis=0, keepdims=True)
        return carry

    lax.fori_loop(0, cells, finish, 0, unroll=2)
    d_hi, d_lo = split(dens[...])
    projected = dot(d_hi, restrict[...]) + dot(d_lo, restrict[...])
    rows = jnp.concatenate([projected[:half], projected[half:]], axis=1)
    own[...] = rows
    rows_all[d] = rows

    def send_rows(k, carry):
        rows_copy(k).start()
        return carry

    lax.fori_loop(1, n, send_rows, 0)

    def store(c, carry):
        adj[c] = it[c].astype(BF16)
        return carry

    lax.fori_loop(0, cells, store, 0, unroll=2)
    early_all[d] = early[...]

    def wait_early(k, carry):
        early_copy(k).wait()
        return carry

    lax.fori_loop(1, n, wait_early, 0)

    tcols[...] = jnp.zeros_like(tcols)

    def take_row(e, carry):
        tcols[pl.ds(e, 1), :] = early_all[e, phalf : phalf + 1, :]
        return carry

    lax.fori_loop(0, n, take_row, 0)
    tturn[...] = jnp.transpose(tcols[...])
    lane1 = lax.broadcasted_iota(jnp.int32, (1, LANES), 1)

    def spot(e, at):
        row = early_all[e, phalf : phalf + 1, :]
        return jnp.sum(jnp.where(lane1 == at, row, 0.0), axis=1, keepdims=True)

    wanted = early_all[d, phalf : phalf + 1, :]
    wanted = jnp.where(lane1 == cells, spot(jnp.maximum(d - 1, 0), cells - 1), wanted)
    wanted = jnp.where(lane1 == cells + 1, spot(jnp.minimum(d + 1, n - 1), 0), wanted)
    wanted = jnp.where(lane1 >= prow, (d * prow + lane1 - prow).astype(F32), wanted)
    for e in range(n):
        rows_e = pl.ds(e * half, half)
        mt_lo[rows_e, :] = (tturn[:half, e : e + 1] == wanted).astype(F32)
        mt_hi[rows_e, :] = (tturn[half : 2 * half, e : e + 1] == wanted).astype(F32)
    wanted_i = wanted.astype(jnp.int32)
    slot = wanted_i % prow
    spread = (wanted_i // prow) * phalf + slot % phalf
    hit = lax.broadcasted_iota(jnp.int32, (n * phalf, LANES), 0) == spread
    table = early_all[:, :phalf, :].reshape(n * phalf, LANES)
    t_hi, t_lo = split(table)
    hit_lo = jnp.where(hit & (slot < phalf), 1.0, 0.0).astype(BF16)
    hit_hi = jnp.where(hit & (slot >= phalf), 1.0, 0.0).astype(BF16)
    pot_rows = dot_first(hit_lo, t_hi) + dot_first(hit_lo, t_lo)
    pot_rows = pot_rows + pltpu.roll(dot_first(hit_hi, t_hi) + dot_first(hit_hi, t_lo), LANES // 2, 1)

    def wait_rows(k, carry):
        rows_copy(k).wait()
        return carry

    lax.fori_loop(1, n, wait_rows, 0)
    g_hi, g_lo = split(rows_all[...].reshape(n * half, LANES))
    m_lo, m_hi = mt_lo[...].astype(BF16), mt_hi[...].astype(BF16)
    total = dot_first(m_lo, g_hi) + dot_first(m_lo, g_lo)
    total = total + pltpu.roll(dot_first(m_hi, g_hi) + dot_first(m_hi, g_lo), LANES // 2, 1)
    lane64 = lax.broadcasted_iota(jnp.int32, (prow, LANES), 1)
    mine = jnp.where(lane64 < coarse, total[:prow], pltpu.roll(total[prow:], LANES // 2, 1))
    packed[...] = mine
    for k in range(1, ranks):
        rank_copy(k).start()
    for k in range(1, ranks):
        rank_copy(k).wait()
        mine = mine + packed_in[k]
    upd[...] = pot[...] - step_rate * pltpu.roll(mine, LANES // 2, 1)[:, :coarse]
    c_hi, c_lo = split((pot_rows[:prow] - step_rate * mine)[:, :coarse])
    node[...] = dot(c_hi, prolong[...]) + dot(c_lo, prolong[...])

    def value0(c):
        return kin[c, :, :LANES] + node[pl.ds(c, 1), :][:, :LANES] * psi[c, :, :LANES].astype(F32)

    def value3(c):
        return kin[c, :, last:] + node[pl.ds(c, 1), :][:, last:] * psi[c, :, last:].astype(F32)

    def middle(c, carry):
        app[c, :, LANES:last] = (
            kin[c, :, LANES:last] + node[pl.ds(c, 1), :][:, LANES:last] * psi[c, :, LANES:last].astype(F32)
        ).astype(BF16)
        return carry

    lax.fori_loop(0, cells, middle, 0, unroll=4)

    def joint(c, carry):
        t0, t3 = value0(c + 1), value3(c)
        y = turned(jnp.where(low, t0, t3), idx[pl.ds(c, 1), :])
        app[c + 1, :, :LANES] = (t0 + jnp.where(low, y, 0.0)).astype(BF16)
        app[c, :, last:] = (t3 + jnp.where(low, 0.0, y)).astype(BF16)
        return carry

    lax.fori_loop(0, end, joint, 0, unroll=2)
    app[0, :, :LANES] = value0(0).astype(BF16)
    app[end, :, last:] = value3(end).astype(BF16)

    @pl.when(has_left)
    def _():
        x_right.wait_recv()
        far = ex_l[:orbs] + node[cells : cells + 1, last:] * ex_l[orbs : 2 * orbs]
        y = turned(far, ex_l[2 * orbs : 2 * orbs + 1].astype(jnp.int32))
        app[0, :, :LANES] = (value0(0) + jnp.where(low, y, 0.0)).astype(BF16)

    @pl.when(has_right)
    def _():
        x_left.wait_recv()
        far = ex_r[:orbs] + node[cells + 1 : cells + 2, :LANES] * ex_r[orbs:]
        y = turned(far, idx[end : end + 1, :])
        app[end, :, last:] = (value3(end) + jnp.where(low, 0.0, y)).astype(BF16)

    @pl.when(has_left)
    def _():
        x_left.wait_send()
        for t in range(ITERS):
            to_left(t).wait_send()

    @pl.when(has_right)
    def _():
        x_right.wait_send()
        for t in range(ITERS):
            to_right(t).wait_send()


def local(
    n,
    ranks,
    orbitals,
    adjoint_source,
    eigenvalues,
    cell_scale,
    base_potential,
    stiffness,
    face_perm,
    restrict,
    prolong,
    owner,
    pot_slot,
    potential,
):
    cells, orbs, nodes = orbitals.shape
    faces = face_perm.shape[1]
    prow, coarse = potential.shape
    count = jnp.arange(faces, dtype=jnp.int32)
    inverse = jnp.sum(jnp.where(face_perm[:, :, None] == count[None, None, :], count[None, :, None], 0), axis=1)
    idx = jnp.concatenate([inverse + faces, face_perm], axis=1)
    target = (owner[:, 0] * prow + pot_slot).astype(F32)
    target = jnp.broadcast_to(jnp.pad(target, (0, LANES - cells))[None], (8, LANES))
    early = jnp.concatenate(
        [jnp.concatenate([potential[: prow // 2], potential[prow // 2 :]], axis=1), target], axis=0
    )
    vmem = pl.BlockSpec(memory_space=pltpu.VMEM)
    smem = pl.BlockSpec(memory_space=pltpu.SMEM)
    dma = pltpu.SemaphoreType.DMA
    half = cells // 2
    face = (orbs, LANES)
    return pl.pallas_call(
        functools.partial(kernel, n, ranks),
        out_shape=(
            jax.ShapeDtypeStruct(orbitals.shape, BF16),
            jax.ShapeDtypeStruct(potential.shape, F32),
            jax.ShapeDtypeStruct(orbitals.shape, BF16),
        ),
        in_specs=[vmem, vmem, vmem, smem, vmem, vmem, vmem, vmem, vmem, vmem, vmem],
        out_specs=(vmem, vmem, vmem),
        scratch_shapes=[
            pltpu.VMEM((cells, orbs, nodes), F32),
            pltpu.VMEM((cells, orbs, nodes), F32),
            pltpu.VMEM((cells,) + face, F32),
            pltpu.VMEM((cells,) + face, F32),
            pltpu.VMEM((cells, nodes), F32),
            pltpu.VMEM((ITERS,) + face, F32),
            pltpu.VMEM((ITERS,) + face, F32),
            pltpu.VMEM((ITERS,) + face, F32),
            pltpu.VMEM((ITERS,) + face, F32),
            pltpu.VMEM((2 * orbs, LANES), F32),
            pltpu.VMEM((2 * orbs + 8, LANES), F32),
            pltpu.VMEM((2 * orbs + 8, LANES), F32),
            pltpu.VMEM((2 * orbs, LANES), F32),
            pltpu.VMEM((n, prow // 2 + 8, LANES), F32),
            pltpu.VMEM((n, half, LANES), F32),
            pltpu.VMEM((half, LANES), F32),
            pltpu.VMEM((n * half, LANES), F32),
            pltpu.VMEM((n * half, LANES), F32),
            pltpu.VMEM((LANES, LANES), F32),
            pltpu.VMEM((LANES, LANES), F32),
            pltpu.VMEM((prow, LANES), F32),
            pltpu.VMEM((ranks, prow, LANES), F32),
            pltpu.VMEM((prow, nodes), F32),
            dma((ITERS,)),
            dma((ITERS,)),
            dma((ITERS,)),
            dma((ITERS,)),
            dma((2,)),
            dma((2,)),
            dma((n,)),
            dma((n,)),
            dma((n,)),
            dma((n,)),
            dma((ranks,)),
            dma((ranks,)),
        ],
        compiler_params=pltpu.CompilerParams(collective_id=0, has_side_effects=True),
    )(
        orbitals,
        adjoint_source,
        eigenvalues[:, None],
        cell_scale,
        base_potential,
        stiffness,
        idx,
        early,
        restrict,
        prolong,
        potential,
    )


def solution(mesh):
    in_specs = (
        P("dom", "orb", None),
        P("dom", "orb", None),
        P("orb"),
        P("dom"),
        P("dom", None),
        P(),
        P("dom", None),
        P(),
        P(),
        P("dom", None),
        P("dom"),
        P("dom", None),
    )
    out_specs = (P("dom", "orb", None), P("dom", None), P("dom", "orb", None))
    step = functools.partial(local, mesh.shape["dom"], mesh.shape["orb"])
    return jax.shard_map(step, mesh=mesh, in_specs=in_specs, out_specs=out_specs, check_vma=False)
```

```python
import functools

import jax
import jax.numpy as jnp
from jax import lax
from jax.experimental import pallas as pl
from jax.experimental.pallas import tpu as pltpu
from jax.sharding import PartitionSpec as P

ITERS = 4


relax = 0.25
step_rate = 0.1

LANES = 128
F32 = jnp.float32
BF16 = jnp.bfloat16


def split(x):
    hi = x.astype(BF16)
    return hi, (x - hi.astype(F32)).astype(BF16)


def dot(a, b):
    return jnp.dot(a, b, preferred_element_type=F32)


def dot_first(a, b):
    return lax.dot_general(a, b, (((0,), (0,)), ((), ())), preferred_element_type=F32)


def dot_last(a, b):
    return lax.dot_general(a, b, (((1,), (1,)), ((), ())), preferred_element_type=F32)


def kernel(
    n,
    ranks,
    psi_any,
    src_any,
    eigs,
    scale,
    base,
    stiff,
    perm,
    owner,
    slots,
    restrict,
    prolong,
    pot,
    adj_any,
    upd,
    app_any,
    psi,
    src,
    adj,
    app,
    idx,
    eig,
    early,
    it,
    kin,
    face0,
    face3,
    dens,
    tx_l,
    tx_r,
    rx_l,
    rx_r,
    ex_tl,
    ex_tr,
    ex_l,
    ex_r,
    early_all,
    rows_all,
    own,
    mt_lo,
    mt_hi,
    tcols,
    tturn,
    packed,
    packed_in,
    node,
    hs_l,
    hs_r,
    hr_l,
    hr_r,
    xs,
    xr,
    es,
    er,
    ps,
    pr,
    ws,
    wr,
    ins,
    outs,
):
    cells, orbs, nodes = psi.shape
    end = cells - 1
    faces = perm.shape[1]
    half = cells // 2
    prow = pot.shape[0]
    phalf = prow // 2
    coarse = pot.shape[1]
    last = nodes - LANES
    d = lax.axis_index("dom")
    r = lax.axis_index("orb")
    barrier = pltpu.get_barrier_semaphore()
    src_copies = [
        pltpu.make_async_copy(src_any.at[pl.ds(a, m)], src.at[pl.ds(a, m)], ins.at[k])
        for k, (a, m) in enumerate(((0, 1), (end, 1), (1, end - 1)))
    ]
    psi_copy = pltpu.make_async_copy(psi_any, psi, ins.at[3])
    for copy in src_copies:
        copy.start()
    psi_copy.start()

    def greet_dom(k, carry):
        pl.semaphore_signal(barrier, inc=1, device_id={"dom": lax.rem(d + k, n)}, device_id_type=pl.DeviceIdType.MESH)
        return carry

    def greet_orb(k, carry):
        pl.semaphore_signal(barrier, inc=1, device_id={"orb": lax.rem(r + k, ranks)}, device_id_type=pl.DeviceIdType.MESH)
        return carry

    lax.fori_loop(1, n, greet_dom, 0)
    lax.fori_loop(1, ranks, greet_orb, 0)

    def send(source, target, s, t, where):
        return pltpu.make_async_remote_copy(
            src_ref=source,
            dst_ref=target,
            send_sem=s,
            recv_sem=t,
            device_id=where,
            device_id_type=pl.DeviceIdType.MESH,
        )

    right = {"dom": jnp.minimum(d + 1, n - 1)}
    left = {"dom": jnp.maximum(d - 1, 0)}
    has_right = d < n - 1
    has_left = d > 0

    def to_left(t):
        return send(tx_l.at[t], rx_r.at[t], hs_l.at[t], hr_r.at[t], left)

    def to_right(t):
        return send(tx_r.at[t], rx_l.at[t], hs_r.at[t], hr_l.at[t], right)

    x_left = send(ex_tl, ex_r, xs.at[0], xr.at[0], left)
    x_right = send(ex_tr, ex_l, xs.at[1], xr.at[1], right)

    def early_copy(k):
        return send(early, early_all.at[d], es.at[k], er.at[k], {"dom": lax.rem(d + k, n)})

    def rows_copy(k):
        return send(own, rows_all.at[d], ps.at[k], pr.at[k], {"dom": lax.rem(d + k, n)})

    def rank_copy(k):
        return send(packed, packed_in.at[k], ws.at[k], wr.at[k], {"orb": lax.rem(r + k, ranks)})

    lane = lax.broadcasted_iota(jnp.int32, (orbs, LANES), 1)
    low = lane < LANES // 2

    def turned(x, row):
        return jnp.take_along_axis(x, jnp.broadcast_to(row, (orbs, LANES)), axis=1)

    group = 8 if cells % 8 == 0 else 1

    row0 = lax.broadcasted_iota(jnp.int32, (orbs, 1), 0)
    column = jnp.zeros((orbs, 1), F32)
    for o in range(orbs):
        column = jnp.where(row0 == o, eigs[o], column)
    eig[...] = column
    lane1 = lax.broadcasted_iota(jnp.int32, (1, LANES), 1)
    tcols[...] = jnp.zeros_like(tcols)
    tcols[:cells, :faces] = perm[...].astype(F32)
    tturn[...] = jnp.transpose(tcols[...])
    place = lax.broadcasted_iota(jnp.int32, (faces, LANES), 0).astype(F32)
    inverse = jnp.zeros((faces, LANES), F32)
    for k in range(faces):
        inverse = jnp.where(place == tturn[k : k + 1, :], float(k), inverse)
    tturn[:faces] = inverse
    tturn[faces:] = tturn[faces:] * 0.0
    inverse = jnp.transpose(tturn[...])[:cells]
    lanes = lax.broadcasted_iota(jnp.int32, (cells, LANES), 1)
    both = jnp.where(lanes < faces, inverse + faces, pltpu.roll(tcols[:cells], faces, 1))
    idx[...] = both.astype(jnp.int32)

    def apply_group(g, carry):
        block = psi[pl.ds(g * group, group)].astype(F32).reshape(group * orbs, nodes).astype(BF16)
        product = dot(block, stiff[...])
        for k in range(group):
            c = g * group + k
            part = product[k * orbs : (k + 1) * orbs]
            kin[c] = scale[c] * part + base[pl.ds(c, 1), :] * psi[c].astype(F32)
        return carry

    def step_group(first, g, carry):
        block = relax * src[pl.ds(g * group, group)].astype(F32) if first else it[pl.ds(g * group, group)]
        block = block.reshape(group * orbs, nodes).astype(BF16)
        product = dot(block, stiff[...])
        for k in range(group):
            c = g * group + k
            value = relax * src[c].astype(F32) if first else it[c]
            part = scale[c] * product[k * orbs : (k + 1) * orbs] + (base[pl.ds(c, 1), :] - eig[...]) * value
            it[c] = value + relax * (src[c].astype(F32) - part)
            face0[c] = part[:, :LANES]
            face3[c] = part[:, last:]
        return carry

    def inner_face(c, carry):
        y = turned(jnp.where(low, face0[c + 1], face3[c]), idx[pl.ds(c, 1), :])
        it[c + 1, :, :LANES] = it[c + 1, :, :LANES] - relax * jnp.where(low, y, 0.0)
        it[c, :, last:] = it[c, :, last:] - relax * jnp.where(low, 0.0, y)
        return carry

    shares = -(-(n - 1) // max(1, ITERS - 1))
    for t in range(ITERS):
        if t == 0:
            src_copies[0].wait()
            src_copies[1].wait()
        edge = relax * src[0].astype(F32) if t == 0 else it[0]
        tx_l[t] = scale[0] * dot(edge.astype(BF16), stiff[:, :LANES]) + (base[0:1, :LANES] - eig[...]) * edge[:, :LANES]
        edge = relax * src[end].astype(F32) if t == 0 else it[end]
        part = scale[end] * dot(edge.astype(BF16), stiff[:, last:]) + (base[end : end + 1, last:] - eig[...]) * edge[:, last:]
        tx_r[t] = turned(part, idx[end : end + 1, :])
        if t == 0:
            row = jnp.zeros((1, LANES), jnp.int32)
            for c in range(cells):
                row = jnp.where(lane1 == c, owner[c] * prow + slots[c], row)
            early[:phalf] = jnp.concatenate([pot[:phalf], pot[phalf:]], axis=1)
            early[phalf:] = jnp.broadcast_to(row.astype(F32), (8, LANES))
            pl.semaphore_wait(barrier, n - 1 + ranks - 1)

        @pl.when(has_left)
        def _():
            to_left(t).start()

        @pl.when(has_right)
        def _():
            to_right(t).start()

        def send_early(k, carry):
            early_copy(k).start()
            return carry

        lax.fori_loop(min(n, 1 + t * shares), min(n, 1 + (t + 1) * shares), send_early, 0)
        if t == 0:
            src_copies[2].wait()
        lax.fori_loop(0, cells // group, functools.partial(step_group, t == 0), 0)
        lax.fori_loop(0, end, inner_face, 0, unroll=2)
        if t == 0:
            psi_copy.wait()
            lax.fori_loop(0, cells // group, apply_group, 0)
            ex_tl[:orbs] = kin[0, :, :LANES]
            ex_tl[orbs:] = psi[0].astype(F32)[:, :LANES]
            ex_tr[:orbs] = kin[end, :, last:]
            ex_tr[orbs : 2 * orbs] = psi[end].astype(F32)[:, last:]
            ex_tr[2 * orbs :] = jnp.broadcast_to(idx[end : end + 1, :], (8, LANES)).astype(F32)

            @pl.when(has_left)
            def _():
                x_left.start()

            @pl.when(has_right)
            def _():
                x_right.start()

        @pl.when(has_left)
        def _():
            to_right(t).wait_recv()
            it[0, :, :LANES] = it[0, :, :LANES] - relax * jnp.where(low, rx_l[t], 0.0)

        @pl.when(has_right)
        def _():
            to_left(t).wait_recv()
            y = turned(rx_r[t], idx[end : end + 1, :])
            it[end, :, last:] = it[end, :, last:] - relax * jnp.where(low, 0.0, y)

    def finish(c, carry):
        dens[pl.ds(c, 1), :] = jnp.sum(psi[c].astype(F32) * it[c], axis=0, keepdims=True)
        return carry

    lax.fori_loop(0, cells, finish, 0, unroll=2)
    d_hi, d_lo = split(dens[...])
    projected = dot_last(d_hi, restrict[...]) + dot_last(d_lo, restrict[...])
    rows = jnp.concatenate([projected[:half], projected[half:]], axis=1)
    own[...] = rows
    rows_all[d] = rows

    def send_rows(k, carry):
        rows_copy(k).start()
        return carry

    lax.fori_loop(1, n, send_rows, 0)

    def store(c, carry):
        adj[c] = it[c].astype(BF16)
        return carry

    lax.fori_loop(0, cells, store, 0, unroll=2)
    adj_copy = pltpu.make_async_copy(adj, adj_any, outs.at[cells // group])
    adj_copy.start()
    early_all[d] = early[...]

    def wait_early(k, carry):
        early_copy(k).wait()
        return carry

    lax.fori_loop(1, n, wait_early, 0)

    tcols[...] = jnp.zeros_like(tcols)

    def take_row(e, carry):
        tcols[pl.ds(e, 1), :] = early_all[e, phalf : phalf + 1, :]
        return carry

    lax.fori_loop(0, n, take_row, 0)
    tturn[...] = jnp.transpose(tcols[...])
    def spot(e, at):
        row = early_all[e, phalf : phalf + 1, :]
        return jnp.sum(jnp.where(lane1 == at, row, 0.0), axis=1, keepdims=True)

    wanted = early_all[d, phalf : phalf + 1, :]
    wanted = jnp.where(lane1 == cells, spot(jnp.maximum(d - 1, 0), cells - 1), wanted)
    wanted = jnp.where(lane1 == cells + 1, spot(jnp.minimum(d + 1, n - 1), 0), wanted)
    wanted = jnp.where(lane1 >= prow, (d * prow + lane1 - prow).astype(F32), wanted)
    for e in range(n):
        rows_e = pl.ds(e * half, half)
        mt_lo[rows_e, :] = (tturn[:half, e : e + 1] == wanted).astype(F32)
        mt_hi[rows_e, :] = (tturn[half : 2 * half, e : e + 1] == wanted).astype(F32)
    wanted_i = wanted.astype(jnp.int32)
    slot = wanted_i % prow
    spread = (wanted_i // prow) * phalf + slot % phalf
    hit = lax.broadcasted_iota(jnp.int32, (n * phalf, LANES), 0) == spread
    table = early_all[:, :phalf, :].reshape(n * phalf, LANES)
    t_hi, t_lo = split(table)
    hit_lo = jnp.where(hit & (slot < phalf), 1.0, 0.0).astype(BF16)
    hit_hi = jnp.where(hit & (slot >= phalf), 1.0, 0.0).astype(BF16)
    pot_rows = dot_first(hit_lo, t_hi) + dot_first(hit_lo, t_lo)
    pot_rows = pot_rows + pltpu.roll(dot_first(hit_hi, t_hi) + dot_first(hit_hi, t_lo), LANES // 2, 1)

    def wait_rows(k, carry):
        rows_copy(k).wait()
        return carry

    lax.fori_loop(1, n, wait_rows, 0)
    g_hi, g_lo = split(rows_all[...].reshape(n * half, LANES))
    m_lo, m_hi = mt_lo[...].astype(BF16), mt_hi[...].astype(BF16)
    total = dot_first(m_lo, g_hi) + dot_first(m_lo, g_lo)
    total = total + pltpu.roll(dot_first(m_hi, g_hi) + dot_first(m_hi, g_lo), LANES // 2, 1)
    lane64 = lax.broadcasted_iota(jnp.int32, (prow, LANES), 1)
    mine = jnp.where(lane64 < coarse, total[:prow], pltpu.roll(total[prow:], LANES // 2, 1))
    packed[...] = mine
    for k in range(1, ranks):
        rank_copy(k).start()
    for k in range(1, ranks):
        rank_copy(k).wait()
        mine = mine + packed_in[k]
    upd[...] = pot[...] - step_rate * pltpu.roll(mine, LANES // 2, 1)[:, :coarse]
    c_hi, c_lo = split((pot_rows[:prow] - step_rate * mine)[:, :coarse])
    node[...] = dot(c_hi, prolong[...]) + dot(c_lo, prolong[...])

    def value0(c):
        return kin[c, :, :LANES] + node[pl.ds(c, 1), :][:, :LANES] * psi[c, :, :LANES].astype(F32)

    def value3(c):
        return kin[c, :, last:] + node[pl.ds(c, 1), :][:, last:] * psi[c, :, last:].astype(F32)

    def middle(c, carry):
        app[c, :, LANES:last] = (
            kin[c, :, LANES:last] + node[pl.ds(c, 1), :][:, LANES:last] * psi[c, :, LANES:last].astype(F32)
        ).astype(BF16)
        return carry

    def joint(c, carry):
        t0, t3 = value0(c + 1), value3(c)
        y = turned(jnp.where(low, t0, t3), idx[pl.ds(c, 1), :])
        app[c + 1, :, :LANES] = (t0 + jnp.where(low, y, 0.0)).astype(BF16)
        app[c, :, last:] = (t3 + jnp.where(low, 0.0, y)).astype(BF16)
        return carry

    app[0, :, :LANES] = value0(0).astype(BF16)
    app[end, :, last:] = value3(end).astype(BF16)

    @pl.when(has_left)
    def _():
        x_right.wait_recv()
        far = ex_l[:orbs] + node[cells : cells + 1, last:] * ex_l[orbs : 2 * orbs]
        y = turned(far, ex_l[2 * orbs : 2 * orbs + 1].astype(jnp.int32))
        app[0, :, :LANES] = (value0(0) + jnp.where(low, y, 0.0)).astype(BF16)

    @pl.when(has_right)
    def _():
        x_left.wait_recv()
        far = ex_r[:orbs] + node[cells + 1 : cells + 2, :LANES] * ex_r[orbs:]
        y = turned(far, idx[end : end + 1, :])
        app[end, :, last:] = (value3(end) + jnp.where(low, 0.0, y)).astype(BF16)

    app_copies = []
    for g in range(cells // group):
        lax.fori_loop(g * group, (g + 1) * group, middle, 0, unroll=2)
        lax.fori_loop(g * group, min(end, (g + 1) * group), joint, 0, unroll=2)
        spread_of = pl.ds(g * group, group)
        app_copies.append(pltpu.make_async_copy(app.at[spread_of], app_any.at[spread_of], outs.at[g]))
        app_copies[g].start()

    @pl.when(has_left)
    def _():
        x_left.wait_send()
        for t in range(ITERS):
            to_left(t).wait_send()

    @pl.when(has_right)
    def _():
        x_right.wait_send()
        for t in range(ITERS):
            to_right(t).wait_send()

    adj_copy.wait()
    for copy in app_copies:
        copy.wait()


def local(
    n,
    ranks,
    orbitals,
    adjoint_source,
    eigenvalues,
    cell_scale,
    base_potential,
    stiffness,
    face_perm,
    restrict,
    prolong,
    owner,
    pot_slot,
    potential,
):
    cells, orbs, nodes = orbitals.shape
    prow = potential.shape[0]
    vmem = pl.BlockSpec(memory_space=pltpu.VMEM)
    smem = pl.BlockSpec(memory_space=pltpu.SMEM)
    hbm = pl.BlockSpec(memory_space=pl.ANY)
    dma = pltpu.SemaphoreType.DMA
    half = cells // 2
    face = (orbs, LANES)
    return pl.pallas_call(
        functools.partial(kernel, n, ranks),
        out_shape=(
            jax.ShapeDtypeStruct(orbitals.shape, BF16),
            jax.ShapeDtypeStruct(potential.shape, F32),
            jax.ShapeDtypeStruct(orbitals.shape, BF16),
        ),
        in_specs=[hbm, hbm, smem, smem, vmem, vmem, vmem, smem, smem, vmem, vmem, vmem],
        out_specs=(hbm, vmem, hbm),
        scratch_shapes=[
            pltpu.VMEM((cells, orbs, nodes), BF16),
            pltpu.VMEM((cells, orbs, nodes), BF16),
            pltpu.VMEM((cells, orbs, nodes), BF16),
            pltpu.VMEM((cells, orbs, nodes), BF16),
            pltpu.VMEM((cells, LANES), jnp.int32),
            pltpu.VMEM((orbs, 1), F32),
            pltpu.VMEM((prow // 2 + 8, LANES), F32),
            pltpu.VMEM((cells, orbs, nodes), F32),
            pltpu.VMEM((cells, orbs, nodes), F32),
            pltpu.VMEM((cells,) + face, F32),
            pltpu.VMEM((cells,) + face, F32),
            pltpu.VMEM((cells, nodes), F32),
            pltpu.VMEM((ITERS,) + face, F32),
            pltpu.VMEM((ITERS,) + face, F32),
            pltpu.VMEM((ITERS,) + face, F32),
            pltpu.VMEM((ITERS,) + face, F32),
            pltpu.VMEM((2 * orbs, LANES), F32),
            pltpu.VMEM((2 * orbs + 8, LANES), F32),
            pltpu.VMEM((2 * orbs + 8, LANES), F32),
            pltpu.VMEM((2 * orbs, LANES), F32),
            pltpu.VMEM((n, prow // 2 + 8, LANES), F32),
            pltpu.VMEM((n, half, LANES), F32),
            pltpu.VMEM((half, LANES), F32),
            pltpu.VMEM((n * half, LANES), F32),
            pltpu.VMEM((n * half, LANES), F32),
            pltpu.VMEM((LANES, LANES), F32),
            pltpu.VMEM((LANES, LANES), F32),
            pltpu.VMEM((prow, LANES), F32),
            pltpu.VMEM((ranks, prow, LANES), F32),
            pltpu.VMEM((prow, nodes), F32),
            dma((ITERS,)),
            dma((ITERS,)),
            dma((ITERS,)),
            dma((ITERS,)),
            dma((2,)),
            dma((2,)),
            dma((n,)),
            dma((n,)),
            dma((n,)),
            dma((n,)),
            dma((ranks,)),
            dma((ranks,)),
            dma((4,)),
            dma((cells + 1,)),
        ],
        compiler_params=pltpu.CompilerParams(collective_id=0, has_side_effects=True),
    )(
        orbitals,
        adjoint_source,
        eigenvalues,
        cell_scale,
        base_potential,
        stiffness,
        face_perm,
        owner[:, 0],
        pot_slot,
        restrict.T,
        prolong,
        potential,
    )


def solution(mesh):
    in_specs = (
        P("dom", "orb", None),
        P("dom", "orb", None),
        P("orb"),
        P("dom"),
        P("dom", None),
        P(),
        P("dom", None),
        P(),
        P(),
        P("dom", None),
        P("dom"),
        P("dom", None),
    )
    out_specs = (P("dom", "orb", None), P("dom", None), P("dom", "orb", None))
    step = functools.partial(local, mesh.shape["dom"], mesh.shape["orb"])
    return jax.shard_map(step, mesh=mesh, in_specs=in_specs, out_specs=out_specs, check_vma=False)
```

```python
import functools

import jax
import jax.numpy as jnp
from jax import lax
from jax.experimental import pallas as pl
from jax.experimental.pallas import tpu as pltpu
from jax.sharding import PartitionSpec as P

ITERS = 4


relax = 0.25
step_rate = 0.1

LANES = 128
F32 = jnp.float32
BF16 = jnp.bfloat16


def split(x):
    hi = x.astype(BF16)
    return hi, (x - hi.astype(F32)).astype(BF16)


def dot(a, b):
    return jnp.dot(a, b, preferred_element_type=F32)


def dot_first(a, b):
    return lax.dot_general(a, b, (((0,), (0,)), ((), ())), preferred_element_type=F32)


def dot_last(a, b):
    return lax.dot_general(a, b, (((1,), (1,)), ((), ())), preferred_element_type=F32)


def kernel(
    n,
    ranks,
    psi_any,
    src_any,
    eigs,
    scale,
    base,
    stiff,
    perm,
    owner,
    slots,
    restrict,
    prolong,
    pot,
    adj,
    upd,
    app,
    psi,
    src,
    idx,
    eig,
    early,
    it,
    kin,
    face0,
    face3,
    dens,
    tx_l,
    tx_r,
    rx_l,
    rx_r,
    ex_tl,
    ex_tr,
    ex_l,
    ex_r,
    early_all,
    rows_all,
    own,
    mt_lo,
    mt_hi,
    tcols,
    tturn,
    packed,
    packed_in,
    node,
    hs_l,
    hs_r,
    hr_l,
    hr_r,
    xs,
    xr,
    es,
    er,
    ps,
    pr,
    ws,
    wr,
    ins,
):
    cells, orbs, nodes = psi.shape
    end = cells - 1
    faces = perm.shape[1]
    half = cells // 2
    prow = pot.shape[0]
    phalf = prow // 2
    coarse = pot.shape[1]
    last = nodes - LANES
    d = lax.axis_index("dom")
    r = lax.axis_index("orb")
    barrier = pltpu.get_barrier_semaphore()
    src_copies = [
        pltpu.make_async_copy(src_any.at[pl.ds(a, m)], src.at[pl.ds(a, m)], ins.at[k])
        for k, (a, m) in enumerate(((0, 1), (end, 1), (1, end - 1)))
    ]
    psi_copy = pltpu.make_async_copy(psi_any, psi, ins.at[3])
    for copy in src_copies:
        copy.start()
    psi_copy.start()

    def greet_dom(k, carry):
        pl.semaphore_signal(barrier, inc=1, device_id={"dom": lax.rem(d + k, n)}, device_id_type=pl.DeviceIdType.MESH)
        return carry

    def greet_orb(k, carry):
        pl.semaphore_signal(barrier, inc=1, device_id={"orb": lax.rem(r + k, ranks)}, device_id_type=pl.DeviceIdType.MESH)
        return carry

    lax.fori_loop(1, n, greet_dom, 0)
    lax.fori_loop(1, ranks, greet_orb, 0)

    def send(source, target, s, t, where):
        return pltpu.make_async_remote_copy(
            src_ref=source,
            dst_ref=target,
            send_sem=s,
            recv_sem=t,
            device_id=where,
            device_id_type=pl.DeviceIdType.MESH,
        )

    right = {"dom": jnp.minimum(d + 1, n - 1)}
    left = {"dom": jnp.maximum(d - 1, 0)}
    has_right = d < n - 1
    has_left = d > 0

    def to_left(t):
        return send(tx_l.at[t], rx_r.at[t], hs_l.at[t], hr_r.at[t], left)

    def to_right(t):
        return send(tx_r.at[t], rx_l.at[t], hs_r.at[t], hr_l.at[t], right)

    x_left = send(ex_tl, ex_r, xs.at[0], xr.at[0], left)
    x_right = send(ex_tr, ex_l, xs.at[1], xr.at[1], right)

    def early_copy(k):
        return send(early, early_all.at[d], es.at[k], er.at[k], {"dom": lax.rem(d + k, n)})

    def rows_copy(k):
        return send(own, rows_all.at[d], ps.at[k], pr.at[k], {"dom": lax.rem(d + k, n)})

    def rank_copy(k):
        return send(packed, packed_in.at[k], ws.at[k], wr.at[k], {"orb": lax.rem(r + k, ranks)})

    lane = lax.broadcasted_iota(jnp.int32, (orbs, LANES), 1)
    low = lane < LANES // 2

    def turned(x, row):
        return jnp.take_along_axis(x, jnp.broadcast_to(row, (orbs, LANES)), axis=1)

    group = 8 if cells % 8 == 0 else 1

    row0 = lax.broadcasted_iota(jnp.int32, (orbs, 1), 0)
    column = jnp.zeros((orbs, 1), F32)
    for o in range(orbs):
        column = jnp.where(row0 == o, eigs[o], column)
    eig[...] = column
    lane1 = lax.broadcasted_iota(jnp.int32, (1, LANES), 1)
    tcols[...] = jnp.zeros_like(tcols)
    tcols[:cells, :faces] = perm[...].astype(F32)
    tturn[...] = jnp.transpose(tcols[...])
    place = lax.broadcasted_iota(jnp.int32, (faces, LANES), 0).astype(F32)
    inverse = jnp.zeros((faces, LANES), F32)
    for k in range(faces):
        inverse = jnp.where(place == tturn[k : k + 1, :], float(k), inverse)
    tturn[:faces] = inverse
    tturn[faces:] = tturn[faces:] * 0.0
    inverse = jnp.transpose(tturn[...])[:cells]
    lanes = lax.broadcasted_iota(jnp.int32, (cells, LANES), 1)
    both = jnp.where(lanes < faces, inverse + faces, pltpu.roll(tcols[:cells], faces, 1))
    idx[...] = both.astype(jnp.int32)

    def apply_group(g, carry):
        block = psi[pl.ds(g * group, group)].astype(F32).reshape(group * orbs, nodes).astype(BF16)
        product = dot(block, stiff[...])
        for k in range(group):
            c = g * group + k
            part = product[k * orbs : (k + 1) * orbs]
            kin[c] = scale[c] * part + base[pl.ds(c, 1), :] * psi[c].astype(F32)
        return carry

    def step_group(first, g, carry):
        block = relax * src[pl.ds(g * group, group)].astype(F32) if first else it[pl.ds(g * group, group)]
        block = block.reshape(group * orbs, nodes).astype(BF16)
        product = dot(block, stiff[...])
        for k in range(group):
            c = g * group + k
            value = relax * src[c].astype(F32) if first else it[c]
            part = scale[c] * product[k * orbs : (k + 1) * orbs] + (base[pl.ds(c, 1), :] - eig[...]) * value
            it[c] = value + relax * (src[c].astype(F32) - part)
            face0[c] = part[:, :LANES]
            face3[c] = part[:, last:]
        return carry

    def inner_faces(start, count):
        at = [start + k for k in range(count)]
        ys = [turned(jnp.where(low, face0[c + 1], face3[c]), idx[pl.ds(c, 1), :]) for c in at]
        lefts = [it[c + 1, :, :LANES] for c in at]
        rights = [it[c, :, last:] for c in at]
        for c, y, a, b in zip(at, ys, lefts, rights):
            it[c + 1, :, :LANES] = a - relax * jnp.where(low, y, 0.0)
            it[c, :, last:] = b - relax * jnp.where(low, 0.0, y)

    def inner_group(g, carry):
        inner_faces(g * group, group)
        return carry

    shares = -(-(n - 1) // max(1, ITERS - 1))
    for t in range(ITERS):
        if t == 0:
            src_copies[0].wait()
            src_copies[1].wait()
        edge = relax * src[0].astype(F32) if t == 0 else it[0]
        tx_l[t] = scale[0] * dot(edge.astype(BF16), stiff[:, :LANES]) + (base[0:1, :LANES] - eig[...]) * edge[:, :LANES]
        edge = relax * src[end].astype(F32) if t == 0 else it[end]
        part = scale[end] * dot(edge.astype(BF16), stiff[:, last:]) + (base[end : end + 1, last:] - eig[...]) * edge[:, last:]
        tx_r[t] = turned(part, idx[end : end + 1, :])
        if t == 0:
            row = jnp.zeros((1, LANES), jnp.int32)
            for c in range(cells):
                row = jnp.where(lane1 == c, owner[c] * prow + slots[c], row)
            early[:phalf] = jnp.concatenate([pot[:phalf], pot[phalf:]], axis=1)
            early[phalf:] = jnp.broadcast_to(row.astype(F32), (8, LANES))
            pl.semaphore_wait(barrier, n - 1 + ranks - 1)

        @pl.when(has_left)
        def _():
            to_left(t).start()

        @pl.when(has_right)
        def _():
            to_right(t).start()

        def send_early(k, carry):
            early_copy(k).start()
            return carry

        lax.fori_loop(min(n, 1 + t * shares), min(n, 1 + (t + 1) * shares), send_early, 0)
        if t == 0:
            src_copies[2].wait()
        lax.fori_loop(0, cells // group, functools.partial(step_group, t == 0), 0)
        lax.fori_loop(0, end // group, inner_group, 0)
        if end % group:
            inner_faces(end - end % group, end % group)
        if t == 0:
            psi_copy.wait()
            lax.fori_loop(0, cells // group, apply_group, 0)
            ex_tl[:orbs] = kin[0, :, :LANES]
            ex_tl[orbs:] = psi[0].astype(F32)[:, :LANES]
            ex_tr[:orbs] = kin[end, :, last:]
            ex_tr[orbs : 2 * orbs] = psi[end].astype(F32)[:, last:]
            ex_tr[2 * orbs :] = jnp.broadcast_to(idx[end : end + 1, :], (8, LANES)).astype(F32)

            @pl.when(has_left)
            def _():
                x_left.start()

            @pl.when(has_right)
            def _():
                x_right.start()

        @pl.when(has_left)
        def _():
            to_right(t).wait_recv()
            it[0, :, :LANES] = it[0, :, :LANES] - relax * jnp.where(low, rx_l[t], 0.0)

        @pl.when(has_right)
        def _():
            to_left(t).wait_recv()
            y = turned(rx_r[t], idx[end : end + 1, :])
            it[end, :, last:] = it[end, :, last:] - relax * jnp.where(low, 0.0, y)

    def finish(c, carry):
        dens[pl.ds(c, 1), :] = jnp.sum(psi[c].astype(F32) * it[c], axis=0, keepdims=True)
        return carry

    lax.fori_loop(0, cells, finish, 0, unroll=4)
    d_hi, d_lo = split(dens[...])
    projected = dot_last(d_hi, restrict[...]) + dot_last(d_lo, restrict[...])
    rows = jnp.concatenate([projected[:half], projected[half:]], axis=1)
    own[...] = rows
    rows_all[d] = rows

    def send_rows(k, carry):
        rows_copy(k).start()
        return carry

    lax.fori_loop(1, n, send_rows, 0)

    def store(c, carry):
        adj[c] = it[c].astype(BF16)
        return carry

    lax.fori_loop(0, cells, store, 0, unroll=4)
    early_all[d] = early[...]

    def wait_early(k, carry):
        early_copy(k).wait()
        return carry

    lax.fori_loop(1, n, wait_early, 0)

    tcols[...] = jnp.zeros_like(tcols)

    def take_row(e, carry):
        tcols[pl.ds(e, 1), :] = early_all[e, phalf : phalf + 1, :]
        return carry

    lax.fori_loop(0, n, take_row, 0)
    tturn[...] = jnp.transpose(tcols[...])
    def spot(e, at):
        row = early_all[e, phalf : phalf + 1, :]
        return jnp.sum(jnp.where(lane1 == at, row, 0.0), axis=1, keepdims=True)

    wanted = early_all[d, phalf : phalf + 1, :]
    wanted = jnp.where(lane1 == cells, spot(jnp.maximum(d - 1, 0), cells - 1), wanted)
    wanted = jnp.where(lane1 == cells + 1, spot(jnp.minimum(d + 1, n - 1), 0), wanted)
    wanted = jnp.where(lane1 >= prow, (d * prow + lane1 - prow).astype(F32), wanted)
    for e in range(n):
        rows_e = pl.ds(e * half, half)
        mt_lo[rows_e, :] = (tturn[:half, e : e + 1] == wanted).astype(F32)
        mt_hi[rows_e, :] = (tturn[half : 2 * half, e : e + 1] == wanted).astype(F32)
    wanted_i = wanted.astype(jnp.int32)
    slot = wanted_i % prow
    spread = (wanted_i // prow) * phalf + slot % phalf
    hit = lax.broadcasted_iota(jnp.int32, (n * phalf, LANES), 0) == spread
    table = early_all[:, :phalf, :].reshape(n * phalf, LANES)
    t_hi, t_lo = split(table)
    hit_lo = jnp.where(hit & (slot < phalf), 1.0, 0.0).astype(BF16)
    hit_hi = jnp.where(hit & (slot >= phalf), 1.0, 0.0).astype(BF16)
    pot_rows = dot_first(hit_lo, t_hi) + dot_first(hit_lo, t_lo)
    pot_rows = pot_rows + pltpu.roll(dot_first(hit_hi, t_hi) + dot_first(hit_hi, t_lo), LANES // 2, 1)

    def wait_rows(k, carry):
        rows_copy(k).wait()
        return carry

    lax.fori_loop(1, n, wait_rows, 0)
    g_hi, g_lo = split(rows_all[...].reshape(n * half, LANES))
    m_lo, m_hi = mt_lo[...].astype(BF16), mt_hi[...].astype(BF16)
    total = dot_first(m_lo, g_hi) + dot_first(m_lo, g_lo)
    total = total + pltpu.roll(dot_first(m_hi, g_hi) + dot_first(m_hi, g_lo), LANES // 2, 1)
    lane64 = lax.broadcasted_iota(jnp.int32, (prow, LANES), 1)
    mine = jnp.where(lane64 < coarse, total[:prow], pltpu.roll(total[prow:], LANES // 2, 1))
    packed[...] = mine
    for k in range(1, ranks):
        rank_copy(k).start()
    for k in range(1, ranks):
        rank_copy(k).wait()
        mine = mine + packed_in[k]
    upd[...] = pot[...] - step_rate * pltpu.roll(mine, LANES // 2, 1)[:, :coarse]
    c_hi, c_lo = split((pot_rows[:prow] - step_rate * mine)[:, :coarse])
    node[...] = dot(c_hi, prolong[...]) + dot(c_lo, prolong[...])

    def value0(c):
        return kin[c, :, :LANES] + node[pl.ds(c, 1), :][:, :LANES] * psi[c, :, :LANES].astype(F32)

    def value3(c):
        return kin[c, :, last:] + node[pl.ds(c, 1), :][:, last:] * psi[c, :, last:].astype(F32)

    def middle(c, carry):
        app[c, :, LANES:last] = (
            kin[c, :, LANES:last] + node[pl.ds(c, 1), :][:, LANES:last] * psi[c, :, LANES:last].astype(F32)
        ).astype(BF16)
        return carry

    def joints(start, count):
        at = [start + k for k in range(count)]
        pairs = [(value0(c + 1), value3(c)) for c in at]
        ys = [turned(jnp.where(low, t0, t3), idx[pl.ds(c, 1), :]) for c, (t0, t3) in zip(at, pairs)]
        for c, (t0, t3), y in zip(at, pairs, ys):
            app[c + 1, :, :LANES] = (t0 + jnp.where(low, y, 0.0)).astype(BF16)
            app[c, :, last:] = (t3 + jnp.where(low, 0.0, y)).astype(BF16)

    def joint_group(g, carry):
        joints(g * group, group)
        return carry

    app[0, :, :LANES] = value0(0).astype(BF16)
    app[end, :, last:] = value3(end).astype(BF16)

    @pl.when(has_left)
    def _():
        x_right.wait_recv()
        far = ex_l[:orbs] + node[cells : cells + 1, last:] * ex_l[orbs : 2 * orbs]
        y = turned(far, ex_l[2 * orbs : 2 * orbs + 1].astype(jnp.int32))
        app[0, :, :LANES] = (value0(0) + jnp.where(low, y, 0.0)).astype(BF16)

    @pl.when(has_right)
    def _():
        x_left.wait_recv()
        far = ex_r[:orbs] + node[cells + 1 : cells + 2, :LANES] * ex_r[orbs:]
        y = turned(far, idx[end : end + 1, :])
        app[end, :, last:] = (value3(end) + jnp.where(low, 0.0, y)).astype(BF16)

    lax.fori_loop(0, cells, middle, 0, unroll=4)
    lax.fori_loop(0, end // group, joint_group, 0)
    if end % group:
        joints(end - end % group, end % group)

    @pl.when(has_left)
    def _():
        x_left.wait_send()
        for t in range(ITERS):
            to_left(t).wait_send()

    @pl.when(has_right)
    def _():
        x_right.wait_send()
        for t in range(ITERS):
            to_right(t).wait_send()


def local(
    n,
    ranks,
    orbitals,
    adjoint_source,
    eigenvalues,
    cell_scale,
    base_potential,
    stiffness,
    face_perm,
    restrict,
    prolong,
    owner,
    pot_slot,
    potential,
):
    cells, orbs, nodes = orbitals.shape
    prow = potential.shape[0]
    vmem = pl.BlockSpec(memory_space=pltpu.VMEM)
    smem = pl.BlockSpec(memory_space=pltpu.SMEM)
    hbm = pl.BlockSpec(memory_space=pl.ANY)
    dma = pltpu.SemaphoreType.DMA
    half = cells // 2
    face = (orbs, LANES)
    return pl.pallas_call(
        functools.partial(kernel, n, ranks),
        out_shape=(
            pltpu.VMEM(orbitals.shape, BF16),
            pltpu.VMEM(potential.shape, F32),
            pltpu.VMEM(orbitals.shape, BF16),
        ),
        in_specs=[hbm, hbm, smem, smem, vmem, vmem, vmem, smem, smem, vmem, vmem, vmem],
        out_specs=(vmem, vmem, vmem),
        scratch_shapes=[
            pltpu.VMEM((cells, orbs, nodes), BF16),
            pltpu.VMEM((cells, orbs, nodes), BF16),
            pltpu.VMEM((cells, LANES), jnp.int32),
            pltpu.VMEM((orbs, 1), F32),
            pltpu.VMEM((prow // 2 + 8, LANES), F32),
            pltpu.VMEM((cells, orbs, nodes), F32),
            pltpu.VMEM((cells, orbs, nodes), F32),
            pltpu.VMEM((cells,) + face, F32),
            pltpu.VMEM((cells,) + face, F32),
            pltpu.VMEM((cells, nodes), F32),
            pltpu.VMEM((ITERS,) + face, F32),
            pltpu.VMEM((ITERS,) + face, F32),
            pltpu.VMEM((ITERS,) + face, F32),
            pltpu.VMEM((ITERS,) + face, F32),
            pltpu.VMEM((2 * orbs, LANES), F32),
            pltpu.VMEM((2 * orbs + 8, LANES), F32),
            pltpu.VMEM((2 * orbs + 8, LANES), F32),
            pltpu.VMEM((2 * orbs, LANES), F32),
            pltpu.VMEM((n, prow // 2 + 8, LANES), F32),
            pltpu.VMEM((n, half, LANES), F32),
            pltpu.VMEM((half, LANES), F32),
            pltpu.VMEM((n * half, LANES), F32),
            pltpu.VMEM((n * half, LANES), F32),
            pltpu.VMEM((LANES, LANES), F32),
            pltpu.VMEM((LANES, LANES), F32),
            pltpu.VMEM((prow, LANES), F32),
            pltpu.VMEM((ranks, prow, LANES), F32),
            pltpu.VMEM((prow, nodes), F32),
            dma((ITERS,)),
            dma((ITERS,)),
            dma((ITERS,)),
            dma((ITERS,)),
            dma((2,)),
            dma((2,)),
            dma((n,)),
            dma((n,)),
            dma((n,)),
            dma((n,)),
            dma((ranks,)),
            dma((ranks,)),
            dma((4,)),
        ],
        compiler_params=pltpu.CompilerParams(collective_id=0, has_side_effects=True),
    )(
        orbitals,
        adjoint_source,
        eigenvalues,
        cell_scale,
        base_potential,
        stiffness,
        face_perm,
        owner[:, 0],
        pot_slot,
        restrict.T,
        prolong,
        potential,
    )


def solution(mesh):
    in_specs = (
        P("dom", "orb", None),
        P("dom", "orb", None),
        P("orb"),
        P("dom"),
        P("dom", None),
        P(),
        P("dom", None),
        P(),
        P(),
        P("dom", None),
        P("dom"),
        P("dom", None),
    )
    out_specs = (P("dom", "orb", None), P("dom", None), P("dom", "orb", None))
    step = functools.partial(local, mesh.shape["dom"], mesh.shape["orb"])
    return jax.shard_map(step, mesh=mesh, in_specs=in_specs, out_specs=out_specs, check_vma=False)
```
